32 devices in a mesh: row: 8 (over y, x, core), col: 4 (over z).
Axes of the slice: x: 2, y: 2, z: 4, core: 2. Of those that a mesh axis runs over, the one named last changes fastest.
Arguments:
- amplitudes: bfloat16 [2048, 8, 2048], P('row', None, 'col'), may hold values from -6 to 6
- factors: bfloat16 [16, 2048, 2048], P(None, 'row', 'col'), may hold values from -0.0625 to 0.0625
- virt_irrep: int32 [32], replicated, may hold values from 0 to 1
- occupied_symmetry_label: int32 [200], replicated, may hold values from 0 to 1
- pair_index: int32 [8, 2], replicated, may hold values from 0 to 199
Outputs:
- ladder: bfloat16 [2048, 8, 2048], P('row', None, 'col')
The draws below stay inside these ranges and needn't reach their ends.
All inputs are finite; a program needn't handle non-finite values.
Results may differ from the reference program's by a relative error of at most 0.0049.
Values may be sent and summed in bfloat16 or wider, within the bound.
No kernel may reach another device: no remote copies, remote signals or barrier semaphores. Data moves between devices by JAX's collectives and lax.ppermute only.
A program may use at most 192 MiB of HBM per device.

```python
import jax
import jax.numpy as jnp
from jax import lax

NV = 2048
VB = 64
NOCC = 200
PAIRS = 8
QB = 16
NBLK = 32


def set_ends(drawn, stream_key, least, high):
    index_at = [jax.random.randint(jax.random.fold_in(stream_key, axis), (), 0, length) for axis, length in enumerate(drawn.shape)]
    longest = drawn.shape.index(max(drawn.shape))
    next_to = index_at[:longest] + [(index_at[longest] + 1) % drawn.shape[longest]] + index_at[longest + 1:]
    return drawn.at[tuple(index_at)].set(least).at[tuple(next_to)].set(high)


def block_scale(stream_key, extent, pieces, least, largest):
    def one(dim, parts):
        steps = jax.random.uniform(jax.random.fold_in(jax.random.fold_in(stream_key, 6), dim), (parts,), jnp.float32, least / len(pieces), largest / len(pieces))
        return jnp.repeat(jnp.exp(steps), extent[dim] // parts).reshape((-1,) + (1,) * (len(extent) - dim - 1))

    level = one(*pieces[0])
    for cut in pieces[1:]:
        level = level * one(*cut)
    return level


def normal_values(stream_key, shape, deviation, limit, cuts=(), held_as=jnp.bfloat16):
    result = deviation * jax.random.normal(stream_key, shape, jnp.float32)
    if cuts:
        result = result * block_scale(stream_key, shape, cuts, -0.22, 0.18)
    return jnp.clip(result, -limit, limit).astype(held_as)


def setup_inputs(seed: int = 0) -> dict:
    key_of = jax.random.split(jax.random.key(seed), 6)
    amplitudes = normal_values(key_of[0], (NV, PAIRS, NV), 1.0, 6.0, ((0, 8), (2, 4)))
    factors = normal_values(key_of[1], (QB, NV, NV), (NV * 4) ** -0.5, 0.0625, ((1, 8), (2, 4)))
    virt_irrep = set_ends(jax.random.randint(key_of[2], (NBLK,), 0, 2), jax.random.fold_in(key_of[2], 1), 0, 1).astype(jnp.int32)
    occupied_symmetry_label = set_ends(jax.random.randint(key_of[3], (NOCC,), 0, 2), jax.random.fold_in(key_of[3], 1), 0, 1).astype(jnp.int32)
    pair_index = set_ends(jax.random.randint(key_of[4], (PAIRS, 2), 0, NOCC), jax.random.fold_in(key_of[4], 1), 0, NOCC - 1).astype(jnp.int32)
    return {"amplitudes": amplitudes, "factors": factors, "virt_irrep": virt_irrep, "occupied_symmetry_label": occupied_symmetry_label, "pair_index": pair_index}


def labels(virt_irrep, occupied_symmetry_label, pair_index):
    blocks = jnp.arange(NV, dtype=jnp.int32) // VB
    lab_v = virt_irrep[blocks]
    lab_p = occupied_symmetry_label[pair_index[:, 0]] + occupied_symmetry_label[pair_index[:, 1]]
    grand_total_sum = lab_v[:, None, None] + lab_p[None, :, None] + lab_v[None, None, :]
    return (grand_total_sum % 2 == 0).astype(jnp.float32)


def reference(amplitudes, factors, virt_irrep, occupied_symmetry_label, pair_index):
    allowed = labels(virt_irrep, occupied_symmetry_label, pair_index)
    masked_terms = (amplitudes.astype(jnp.float32) * allowed).astype(jnp.bfloat16).astype(jnp.float32)

    def step(grand_total_sum, factor_q):
        fitted_factor_matrix = factor_q.astype(jnp.float32)
        half_span = jnp.einsum("jmq,qk->jmk", masked_terms, fitted_factor_matrix).astype(jnp.bfloat16).astype(jnp.float32)
        return grand_total_sum + jnp.einsum("sg,srl->grl", fitted_factor_matrix, half_span), None

    start = jnp.zeros((NV, PAIRS, NV), jnp.float32)
    full, _ = lax.scan(step, start, factors)
    return (allowed * full).astype(jnp.bfloat16)
```

```python
import functools

import jax
import jax.numpy as jnp
from jax import lax
from jax.experimental import pallas as pl
from jax.experimental.pallas import tpu as pltpu
from jax.sharding import PartitionSpec as P


VB = 64


def lookup(index_entries, table):
    places = jnp.arange(table.shape[0], dtype=jnp.int32)
    hits = index_entries[..., None] == places
    return jnp.sum(jnp.where(hits, table, 0), axis=-1)


def allowed_here(rows, width, virt_irrep, occupied_symmetry_label, pair_index):
    row_start = lax.axis_index("row") * rows
    col_start = lax.axis_index("col") * width
    row_ids = (row_start + jnp.arange(rows, dtype=jnp.int32)) // VB
    col_ids = (col_start + jnp.arange(width, dtype=jnp.int32)) // VB
    lab_rows = lookup(row_ids, virt_irrep)
    lab_cols = lookup(col_ids, virt_irrep)
    lab_pair = lookup(pair_index[:, 0], occupied_symmetry_label) + lookup(
        pair_index[:, 1], occupied_symmetry_label
    )
    parity = lab_rows[:, None, None] + lab_pair[None, :, None] + lab_cols[None, None, :]
    return parity % 2 == 0


def by_gathers(amplitudes, factors, virt_irrep, occupied_symmetry_label, pair_index):
    rows, pairs, width = amplitudes.shape
    groups = factors.shape[0]
    allowed = allowed_here(rows, width, virt_irrep, occupied_symmetry_label, pair_index)
    masked = jnp.where(allowed, amplitudes, 0)
    panel = lax.all_gather(masked, "col", axis=2, tiled=True)
    flat_panel = panel.reshape(rows * pairs, -1)
    halves = []
    panels = []
    group_size = min(8, groups)
    for first in range(0, groups, group_size):
        block = factors[first : first + group_size]
        summed = jnp.einsum(
            "md,qdb->qmb",
            flat_panel,
            lax.all_gather(block, "row", axis=1, tiled=True),
            preferred_element_type=jnp.float32,
        )
        halves.append(summed.astype(jnp.bfloat16).reshape(group_size, rows, pairs * width))
        panels.append(lax.all_gather(block, "col", axis=2, tiled=True))
    result = jnp.zeros((rows * lax.axis_size("row"), pairs * width), jnp.float32)
    for half_block, panel_block in zip(halves, panels):
        result = result + jnp.einsum(
            "qca,qcn->an", panel_block, half_block, preferred_element_type=jnp.float32
        )
    full = lax.psum_scatter(result, "row", scatter_dimension=0, tiled=True)
    full = full.reshape(rows, pairs, width)
    return jnp.where(allowed, full, 0).astype(jnp.bfloat16)


def swap(value, axis, bit):
    size = lax.axis_size(axis)
    return lax.ppermute(value, axis, [(i, i ^ bit) for i in range(size)])


def pick(value, index, axis=0):
    return lax.dynamic_index_in_dim(value, index, axis, keepdims=False)


def ladder_step(terms_ref, own_ref, got_ref, *refs, first, start, tile):
    acc_ref = None if first else refs[0]
    out_ref, half_ref = refs[-2:]
    side = own_ref.shape[0]
    width = out_ref.shape[1]
    place = pl.multiple_of((pl.program_id(0) + start) * width, width)
    cols = pl.ds(place, width)

    def product(left, right, contract):
        return lax.dot_general(
            left, right, (contract, ((), ())), preferred_element_type=jnp.float32
        )

    def first_half(i, carry):
        rows = pl.ds(pl.multiple_of(i * tile, tile), tile)
        value = product(terms_ref[rows, :side], own_ref[:, cols], ((1,), (0,)))
        value = value + product(terms_ref[rows, side:], got_ref[:, cols], ((1,), (0,)))
        half_ref[rows, :] = value.astype(half_ref.dtype)
        return carry

    def second_half(i, carry):
        rows = pl.ds(pl.multiple_of(i * tile, tile), tile)
        value = product(own_ref[:, rows], half_ref[:side], ((0,), (0,)))
        value = value + product(got_ref[:, rows], half_ref[side:], ((0,), (0,)))
        if not first:
            value = value + acc_ref[rows, :]
        out_ref[rows, :] = value
        return carry

    lax.fori_loop(0, terms_ref.shape[0] // tile, first_half, 0)
    lax.fori_loop(0, out_ref.shape[0] // tile, second_half, 0)


def add_step(terms, own, got, acc, width, start=None):
    size = terms.shape[0]
    whole = start is None
    once = pl.Buffered(1)
    fixed = [
        pl.BlockSpec(array.shape, lambda n: (0, 0), pipeline_mode=once)
        for array in (terms, own, got)
    ]
    first = acc is None
    shift = 0 if whole else start
    moving = [] if first else [pl.BlockSpec((size, width), lambda n: (0, n + shift))]
    return pl.pallas_call(
        functools.partial(ladder_step, first=first, start=shift, tile=width),
        grid=(size // width if whole else 1,),
        in_specs=fixed + moving,
        out_specs=pl.BlockSpec((size, width), lambda n: (0, n)),
        out_shape=jax.ShapeDtypeStruct((size, size if whole else width), jnp.float32),
        scratch_shapes=[pltpu.VMEM((size, width), jnp.bfloat16)],
        input_output_aliases={3: 0} if whole and not first else {},
        compiler_params=pltpu.CompilerParams(vmem_limit_bytes=46 << 20),
        name="ladder_step",
    )(terms, own, got, *([] if first else [acc]))


def by_exchanges(amplitudes, factors, virt_irrep, occupied_symmetry_label, pair_index):
    rows, pairs, width = amplitudes.shape
    groups = factors.shape[0]
    steps = groups // 4
    place = lax.axis_index("row")
    y, x, core = (place >> 2) & 1, (place >> 1) & 1, place & 1
    spot = lax.axis_index("col")
    z1, z0 = (spot >> 1) & 1, spot & 1
    allowed = allowed_here(rows, width, virt_irrep, occupied_symmetry_label, pair_index)
    masked = jnp.where(allowed, amplitudes, 0)

    around = [yr * 4 + xr * 2 + cr for cr in (0, 1) for xr in (0, 1) for yr in (0, 1)]

    def reorder(value):
        flat = value.reshape(-1, 4 * width)
        blocks = []
        for step in around:
            actual = place ^ step
            away = (actual >> 1) ^ spot
            start = ((away & 1) * 2 + (away >> 1)) * width + (actual & 1) * rows
            blocks.append(lax.dynamic_slice_in_dim(flat, start, rows, axis=1))
        return jnp.concatenate(blocks, axis=1).reshape(value.shape)

    by_pair = jnp.transpose(masked, (1, 0, 2)).reshape(2, 2, 2, 2, rows // 2, width)
    near, far = [], []
    for h in (0, 1):
        terms = by_pair[:, :, :, h]
        terms = jnp.stack([pick(terms, core, 2), swap(pick(terms, 1 - core, 2), "row", 1)])
        terms = jnp.stack([pick(terms, y, 1), swap(pick(terms, 1 - y, 1), "row", 4)], axis=1)
        terms = jnp.concatenate(
            [pick(terms, z1, 2), swap(pick(terms, 1 - z1, 2), "col", 2)], axis=-1
        )
        terms = jnp.concatenate([terms, swap(terms, "col", 1)], axis=-1)
        near.append(reorder(terms))
        far.append(reorder(swap(terms, "row", 2)))
    left = jnp.stack(
        [jnp.stack([near[0], near[1]], axis=2), jnp.stack([far[0], far[1]], axis=2)], axis=1
    ).reshape(8 * rows, 4 * width)

    split = factors.reshape(2, 2, steps, rows, width)
    acc = None
    for step in range(steps):
        own = split[:, :, step]
        own = jnp.stack([pick(own, x), swap(pick(own, 1 - x), "row", 2)])
        own = jnp.concatenate([pick(own, z0, 1), swap(pick(own, 1 - z0, 1), "col", 1)], axis=-1)
        own = jnp.concatenate([own, swap(own, "col", 2)], axis=-1)
        own = jnp.stack([own, swap(own, "row", 4)], axis=1)
        own = own.reshape(4 * rows, 4 * width)
        got = swap(own, "row", 1)
        if step + 1 < steps:
            acc = add_step(left, own, got, acc, width)

    sums = {}
    for zr1 in (1, 0):
        for zr0 in (1, 0):
            part = add_step(left, own, got, acc, width, 2 * zr1 + zr0)
            part = part.reshape(2, 2, width, width)
            away = pick(part, (1 - x) ^ z0, 1).astype(jnp.bfloat16)
            away = swap(away, "row", 2)
            sums[zr1, zr0] = pick(part, x ^ z0, 1) + away.astype(jnp.float32)
    parts = []
    for zr1 in (0, 1):
        away = swap(sums[zr1, 1].astype(jnp.bfloat16), "col", 1)
        done = (sums[zr1, 0] + away.astype(jnp.float32)).astype(jnp.bfloat16)
        parts.append(jnp.stack([pick(done, y ^ z1), pick(done, 1 - (y ^ z1))]))
    parts[1] = swap(parts[1], "col", 2)
    for i in (0, 1):
        part = jnp.stack([parts[i][0], swap(parts[i][1], "row", 4)])
        part = part.reshape(2, 2, rows, width)
        parts[i] = jnp.stack([pick(part, core, 1), swap(pick(part, 1 - core, 1), "row", 1)], axis=1)
    both = jnp.stack(parts, axis=1)
    both = jnp.where(y == 1, both[::-1], both)
    both = jnp.where(z1 == 1, both[:, ::-1], both)
    both = jnp.where(core == 1, both[:, :, ::-1], both)
    full = jnp.transpose(both.reshape(pairs, rows, width), (1, 0, 2))
    return jnp.where(allowed, full, 0)


def solution(mesh):
    in_specs = (P("row", None, "col"), P(None, "row", "col"), P(), P(), P())
    out_specs = P("row", None, "col")
    paired = mesh.shape["row"] == 8 and mesh.shape["col"] == 4

    def on_device(*arguments):
        if not paired:
            return by_gathers(*arguments)
        return by_exchanges(*arguments)

    return jax.shard_map(
        on_device, mesh=mesh, in_specs=in_specs, out_specs=out_specs, check_vma=False
    )
```
